32 devices in a mesh: groups: 2 (over y), tile: 4 (over z), sect: 2 (over x), half: 2 (over core).
Axes of the slice: x: 2, y: 2, z: 4, core: 2. Of those that a mesh axis runs over, the one named last changes fastest.
Arguments:
- patches: bfloat16 [4, 4, 32, 256, 256], P(('groups', 'sect'), 'tile', 'half'), parts along dimension 0, may hold values from -6 to 6
- pair_lists: int32 [3, 4, 4, 24], P(None, ('groups', 'sect'), 'tile', 'half'), parts along dimension 1, may hold values from 0 to 15, as said below
- move_plan: int32 [2, 4, 4, 24], P(None, ('groups', 'sect'), 'tile', 'half'), parts along dimension 1, may hold values from -1 to 5, as said below
Outputs:
- work_surfaces: float32 [4, 4, 12, 256, 256], P(('groups', 'sect'), 'tile', 'half'), parts along dimension 0
- peak_values: float32 [4, 4, 24], P(('groups', 'sect'), 'tile', 'half'), parts along dimension 0
The draws below stay inside these ranges and needn't reach their ends.
There are 2 independent parts, one for each index of `groups`. The reference program is written for one: setup_inputs(seed, part) draws one part's arguments, and reference() takes and returns one part's arrays. A program takes and returns all parts, laid end to end along the dimension named above; each array names one. Nothing has to cross between parts.
Inputs may be any that keep to these rules, and one draw needn't show every extreme that they name: `pair_lists`: kind 0 names the tile row below (r + 1), kind 1 the next section (s + 1). Every slot of the last tile row has kind 1 and every slot of the last section kind 0; the device of the last tile row in the last section has no live slot. Entries a and b are below 16. `move_plan`: entry 0 is the target tile row of a slot (-1 for unused), entry 1 its work slot there (-1 for unused). A device has at most 12 live slots and at most 3 live slots with the same target; within one section and column half no two live slots share a target and a work slot, work slots are below 6, and live slots are all assigned. Some device has 12 live slots and some target receives 6.
All inputs are finite; a program needn't handle non-finite values.
Results may differ from the reference program's by a relative error of at most 0.0003.
Values may be sent and summed in bfloat16 or wider, within the bound.
A program may use at most 64 MiB of HBM per device.

```python
import jax
import jax.numpy as jnp
from jax import lax

PS = 256
PATCHES = 16
SLOTS = 12
WORK = 6
TILE_ROWS = 4
SECTIONS = 2


def draw_pair_lists(key, part):
    subkeys = jax.random.split(jax.random.fold_in(key, 11), 3)
    grid_shape = (SECTIONS, TILE_ROWS, 2 * SLOTS)
    pair_kinds = jax.random.randint(subkeys[0], grid_shape, 0, 2)
    sect_ids = jnp.arange(SECTIONS, dtype=jnp.int32)[:, None, None]
    row_ids = jnp.arange(TILE_ROWS, dtype=jnp.int32)[None, :, None]
    pair_kinds = jnp.where(row_ids == TILE_ROWS - 1, 1, pair_kinds)
    pair_kinds = jnp.where(sect_ids == SECTIONS - 1, 0, pair_kinds)
    first_index = jax.random.randint(subkeys[1], grid_shape, 0, PATCHES)
    second_index = jax.random.randint(subkeys[2], grid_shape, 0, PATCHES)
    return jnp.stack([pair_kinds, first_index, second_index]).astype(jnp.int32)


def draw_move_plan(key, part):
    subkeys = jax.random.split(jax.random.fold_in(key, 23), 7)
    columns = SECTIONS * 2
    rows_total = TILE_ROWS
    row_ids = jnp.arange(rows_total, dtype=jnp.int32)
    heavy_row = jax.random.randint(subkeys[0], (columns,), 0, rows_total - 1)
    totals = jax.random.randint(subkeys[1], (columns,), rows_total * (WORK - 1) + 1, rows_total * WORK + 1)
    weights = jax.random.randint(subkeys[2], (columns, rows_total), 1, 4)
    sect_of = jnp.arange(columns, dtype=jnp.int32) // 2
    blocked = (sect_of[:, None] == SECTIONS - 1) & (row_ids[None, :] == rows_total - 1)
    is_heavy = row_ids[None, :] == heavy_row[:, None]
    weights = jnp.where(blocked | is_heavy, 0, weights)
    weight_sum = jnp.maximum(jnp.sum(weights, axis=1, keepdims=True), 1)
    shares = jnp.minimum((totals[:, None] - SLOTS) * weights // weight_sum, SLOTS)
    counts = jnp.where(is_heavy, SLOTS, shares).astype(jnp.int32)
    visit_scores = jax.random.randint(subkeys[3], (columns, rows_total), 0, 1 << 20) * rows_total + row_ids[None, :]
    visits = jnp.argsort(visit_scores, axis=1).astype(jnp.int32)

    def fill_step(step, carried):
        counts_now, leftover = carried
        device_row = visits[:, step]
        onehot = row_ids[None, :] == device_row[:, None]
        spare_room = jnp.sum(jnp.where(onehot & ~blocked, SLOTS - counts_now, 0), axis=1)
        added = jnp.minimum(spare_room, leftover)
        return (counts_now + jnp.where(onehot, added[:, None], 0), leftover - added)
    leftover = totals - jnp.sum(counts, axis=1)
    counts, leftover = lax.fori_loop(0, rows_total, fill_step, (counts, leftover))
    slot_ids = jnp.arange(SLOTS, dtype=jnp.int32)
    scores = jax.random.randint(subkeys[4], (columns, rows_total, SLOTS), 0, 1 << 20) * SLOTS + slot_ids
    ranks = jnp.argsort(jnp.argsort(scores, axis=2), axis=2)
    is_live = ranks < counts[:, :, None]
    before = jnp.cumsum(is_live.astype(jnp.int32), axis=2) - 1
    order_scores = jax.random.randint(subkeys[5], (columns, rows_total), 0, 1 << 20) * rows_total + row_ids[None, :]
    positions = jnp.argsort(jnp.argsort(order_scores, axis=1), axis=1)
    earlier = positions[:, None, :] < positions[:, :, None]
    offset = jnp.sum(jnp.where(earlier, counts[:, None, :], 0), axis=2)
    global_rank = offset[:, :, None] + before
    dest_scores = jax.random.randint(subkeys[6], (columns, rows_total), 0, 1 << 20) * rows_total + row_ids[None, :]
    dest_perm = jnp.argsort(dest_scores, axis=1).astype(jnp.int32)
    residue = (global_rank % rows_total).reshape(columns, rows_total * SLOTS)
    destination = jnp.take_along_axis(dest_perm, residue, axis=1).reshape(columns, rows_total, SLOTS)
    targets = jnp.where(is_live, destination, -1)
    places = jnp.where(is_live, global_rank // rows_total, -1)

    def arrange(values):
        shaped = values.reshape(SECTIONS, 2, rows_total, SLOTS).transpose(0, 2, 1, 3)
        return shaped.reshape(SECTIONS, rows_total, 2 * SLOTS)
    return jnp.stack([arrange(targets), arrange(places)]).astype(jnp.int32)


def block_levels(rng, extent, pieces, smallest, high):
    factor_of, own = 1.0, jax.random.fold_in(rng, 6)
    for position, shards_of in pieces:
        steps = jnp.exp(jax.random.uniform(jax.random.fold_in(own, position), (shards_of,), jnp.float32, smallest / len(pieces), high / len(pieces)))
        factor_of = factor_of * jnp.repeat(steps, extent[position] // shards_of).reshape([-1 if axis == position else 1 for axis in range(len(extent))])
    return factor_of


def gaussian(stream_key, extent, spread, bound, cuts=(), kind=jnp.bfloat16):
    drawn = jax.random.normal(stream_key, extent, jnp.float32) * spread
    if len(cuts) > 0:
        drawn = block_levels(stream_key, extent, cuts, -0.22, 0.18) * drawn
    return jnp.clip(drawn, min=-bound, max=bound).astype(kind)


def setup_inputs(seed: int = 0, part: int = 0) -> dict:
    arg_keys = jax.random.split(jax.random.key(seed), 4)
    part_keys = jax.random.split(jax.random.fold_in(arg_keys[3], part), 4)
    return {
        "patches": gaussian(part_keys[0], (SECTIONS, TILE_ROWS, 2 * PATCHES, PS, PS), 1.0, 6.0, ((0, 2), (1, 4), (2, 2))),
        "pair_lists": draw_pair_lists(jax.random.fold_in(jax.random.fold_in(arg_keys[3], part), 71), part),
        "move_plan": draw_move_plan(jax.random.fold_in(jax.random.fold_in(arg_keys[3], part), 71), part),
    }


FLOOR = 0.05


def surface_of(first_patch, second_patch):
    spec_first = jnp.fft.fft2(first_patch.astype(jnp.float32))
    spec_second = jnp.fft.fft2(second_patch.astype(jnp.float32))
    cross_power = spec_first * jnp.conj(spec_second)
    scaled = cross_power / jnp.maximum(jnp.abs(cross_power), FLOOR * PS * PS)
    return (jnp.real(jnp.fft.ifft2(scaled)) * PS).astype(jnp.float32)


def reference(patches, pair_lists, move_plan):
    halves = 2
    flat_patches = patches.reshape(SECTIONS * TILE_ROWS * halves * PATCHES, PS, PS)
    grid = (SECTIONS, TILE_ROWS, halves, SLOTS)
    sect_ids = jnp.arange(SECTIONS, dtype=jnp.int32)[:, None, None, None]
    row_ids = jnp.arange(TILE_ROWS, dtype=jnp.int32)[None, :, None, None]
    half_ids = jnp.arange(halves, dtype=jnp.int32)[None, None, :, None]
    slot_ids = jnp.arange(SLOTS, dtype=jnp.int32)[None, None, None, :]
    pair_kinds = pair_lists[0].reshape(grid)
    first_index = pair_lists[1].reshape(grid)
    second_index = pair_lists[2].reshape(grid)
    targets = move_plan[0].reshape(grid)
    places = move_plan[1].reshape(grid)
    slot_alive = targets >= 0
    patch_total = SECTIONS * TILE_ROWS * halves * PATCHES
    first_flat = ((sect_ids * TILE_ROWS + row_ids) * halves + half_ids) * PATCHES + first_index
    partner_sect = sect_ids + pair_kinds
    partner_row = row_ids + 1 - pair_kinds
    second_flat = ((partner_sect * TILE_ROWS + partner_row) * halves + half_ids) * PATCHES + second_index
    first_flat = jnp.clip(first_flat, 0, patch_total - 1).astype(jnp.int32)
    second_flat = jnp.clip(second_flat, 0, patch_total - 1).astype(jnp.int32)
    work_total = SECTIONS * TILE_ROWS * halves * WORK
    work_flat = ((sect_ids * TILE_ROWS + targets) * halves + half_ids) * WORK + places
    work_flat = jnp.where(slot_alive, work_flat, work_total).astype(jnp.int32)
    slot_flat = (((sect_ids * TILE_ROWS + row_ids) * halves + half_ids) * SLOTS + slot_ids) + jnp.zeros(grid, jnp.int32)
    source = jnp.full((work_total + 1,), -1, jnp.int32).at[work_flat.reshape(-1)].set(slot_flat.reshape(-1).astype(jnp.int32))[:work_total]
    is_valid = source >= 0
    safe_source = jnp.maximum(source, 0)
    first_pick = first_flat.reshape(-1)[safe_source]
    second_pick = second_flat.reshape(-1)[safe_source]

    def one_entry(entry):
        pick_first, pick_second, valid_entry = entry
        surface = surface_of(flat_patches[pick_first], flat_patches[pick_second])
        return jnp.where(valid_entry, surface, jnp.zeros_like(surface))

    surfaces = lax.map(one_entry, (first_pick, second_pick, is_valid))
    work_peaks = jnp.max(surfaces, axis=(1, 2))
    slot_peaks = work_peaks[jnp.clip(work_flat, 0, work_total - 1).reshape(-1)].reshape(grid)
    peak_values = jnp.where(slot_alive, slot_peaks, jnp.zeros_like(slot_peaks))
    work_surfaces = surfaces.reshape(SECTIONS, TILE_ROWS, halves * WORK, PS, PS)
    return work_surfaces, peak_values.reshape(SECTIONS, TILE_ROWS, halves * SLOTS)
```

```python
import jax
import jax.numpy as jnp
import numpy as np
from jax import lax
from jax.experimental import pallas as pl
from jax.experimental.pallas import tpu as pltpu
from jax.sharding import PartitionSpec as P

FLOOR = 0.05


def passed_along(value, axis, steps):
    count = lax.axis_size(axis)
    leading, last = (max(0, -steps), min(count, count - steps))
    return lax.ppermute(value, axis, [(source, source + steps) for source in range(leading, last)])


def real_tables(length):
    half = length // 2
    spots = np.arange(length)
    waves = np.arange(half)
    angles = (spots[:, None] * waves[None, :] % length) * (2.0 * np.pi / length)
    sines = np.sin(angles)
    sines[:, 0] = np.cos(np.pi * spots)
    table = np.concatenate([np.cos(angles), sines], axis=1).astype(np.float32)
    upper = table.astype(jnp.bfloat16)
    lower = (table - upper.astype(np.float32)).astype(jnp.bfloat16)
    column = np.stack([upper, lower])
    row = np.stack([upper.T, lower.T])
    return jnp.asarray(column), jnp.asarray(row)


def halves_of(value):
    upper = value.astype(jnp.bfloat16)
    return upper, (value - upper.astype(jnp.float32)).astype(jnp.bfloat16)


def dot(left, right):
    return jnp.dot(left, right, preferred_element_type=jnp.float32)


def left_product(table_ref, value):
    upper, lower = halves_of(value)
    return dot(table_ref[0], upper) + dot(table_ref[0], lower) + dot(table_ref[1], upper)


def right_product(value, table_ref):
    upper, lower = halves_of(value)
    return dot(upper, table_ref[0]) + dot(lower, table_ref[0]) + dot(upper, table_ref[1])


def packed_spectrum(picture, column_ref, row_ref):
    across = dot(picture, column_ref[0]) + dot(picture, column_ref[1])
    return left_product(row_ref, across)


def unpacked(packed, on_row, on_column):
    half = packed.shape[0] // 2
    cc, cs = packed[:half, :half], packed[:half, half:]
    sc, ss = packed[half:, :half], packed[half:, half:]
    edge = on_row | on_column
    plus_re = jnp.where(edge, cc, cc - ss)
    plus_im = jnp.where(on_row, cs, jnp.where(on_column, sc, sc + cs))
    minus_re = jnp.where(on_row, sc, jnp.where(on_column, cs, cc + ss))
    minus_im = jnp.where(edge, ss, cs - sc)
    return (plus_re, plus_im, minus_re, minus_im)


def phases(first_re, first_im, second_re, second_im, floor):
    cross_re = first_re * second_re + first_im * second_im
    cross_im = first_re * second_im - first_im * second_re
    power = cross_re * cross_re + cross_im * cross_im
    factor = jnp.minimum(lax.rsqrt(power), 1.0 / floor)
    return (cross_re * factor, cross_im * factor)


def correlate(first, second, column_ref, row_ref):
    length = first.shape[-1]
    half = length // 2
    floor = FLOOR * length * length
    first_packed = packed_spectrum(first, column_ref, row_ref)
    second_packed = packed_spectrum(second, column_ref, row_ref)
    rows = lax.broadcasted_iota(jnp.int32, (half, half), 0)
    columns = lax.broadcasted_iota(jnp.int32, (half, half), 1)
    on_row, on_column = rows == 0, columns == 0
    corner = on_row & on_column
    one = unpacked(first_packed, on_row, on_column)
    two = unpacked(second_packed, on_row, on_column)
    plus_re, plus_im = phases(one[0], one[1], two[0], two[1], floor)
    minus_re, minus_im = phases(one[2], one[3], two[2], two[3], floor)
    cc = jnp.where(on_row | on_column, plus_re, plus_re + minus_re)
    ss = jnp.where(on_row | on_column, -minus_im, minus_re - plus_re)
    sc = jnp.where(on_row, minus_re, jnp.where(on_column, -plus_im, minus_im - plus_im))
    cs = jnp.where(on_row, -plus_im, jnp.where(on_column, minus_re, -plus_im - minus_im))

    def at_corner(value, top, left):
        product = (
            first_packed[top : top + half, left : left + half]
            * second_packed[top : top + half, left : left + half]
        )
        real = product / jnp.maximum(jnp.abs(product), floor)
        return jnp.where(corner, 0.5 * real, value)

    packed = jnp.concatenate(
        [
            jnp.concatenate([at_corner(cc, 0, 0), at_corner(cs, 0, half)], axis=1),
            jnp.concatenate([at_corner(sc, half, 0), at_corner(ss, half, half)], axis=1),
        ],
        axis=0,
    )
    scale = 2.0 / length
    return left_product(column_ref, right_product(packed * scale, row_ref))


def couple_kernel(picks_ref, first_ref, second_ref, column_ref, row_ref, surface_ref, peak_ref):
    step = pl.program_id(0)

    @pl.when(picks_ref[2, step] == 0)
    def _():
        surface_ref[...] = jnp.zeros_like(surface_ref)
        peak_ref[...] = jnp.zeros_like(peak_ref)

    @pl.when(picks_ref[2, step] != 0)
    def _():
        surface = correlate(first_ref[0, 0], second_ref[0, 0], column_ref, row_ref)
        surface_ref[0] = surface
        peak_ref[...] = jnp.full(peak_ref.shape, jnp.max(surface), jnp.float32)


def correlate_all(picks, first_from, second_from, first_lane, second_lane):
    work_count = picks.shape[1]
    length = first_from.shape[-1]
    column, row = real_tables(length)
    whole_table = pl.BlockSpec((2, length, length), lambda w, p: (0, 0, 0))
    surfaces, peaks = pl.pallas_call(
        couple_kernel,
        grid_spec=pltpu.PrefetchScalarGridSpec(
            num_scalar_prefetch=1,
            grid=(work_count,),
            in_specs=[
                pl.BlockSpec((1, 1, length, length), lambda w, p: (p[0, w], first_lane, 0, 0)),
                pl.BlockSpec((1, 1, length, length), lambda w, p: (p[1, w], second_lane, 0, 0)),
                whole_table,
                whole_table,
            ],
            out_specs=[
                pl.BlockSpec((1, length, length), lambda w, p: (w, 0, 0)),
                pl.BlockSpec((1, 1, 128), lambda w, p: (w, 0, 0)),
            ],
        ),
        out_shape=[
            jax.ShapeDtypeStruct((work_count, length, length), jnp.float32),
            jax.ShapeDtypeStruct((work_count, 1, 128), jnp.float32),
        ],
    )(picks, first_from, second_from, column, row)
    return surfaces, peaks[:, 0, 0]


def settle(arrived_place, lane_ids, work_ids):
    matches = arrived_place[None, :] == work_ids[:, None]
    present = jnp.any(matches, axis=1)
    picked = jnp.sum(jnp.where(matches, lane_ids[None, :], 0), axis=1)
    return (present, picked)


def body(patches, pair_lists, move_plan):
    own_patches = patches[0, 0]
    from_below = passed_along(own_patches, "tile", -1)
    from_next = passed_along(own_patches, "sect", -1)
    pair_kinds = pair_lists[0, 0, 0]
    first_index = pair_lists[1, 0, 0]
    second_index = pair_lists[2, 0, 0]
    targets = move_plan[0, 0, 0]
    places = move_plan[1, 0, 0]
    slot_count = pair_kinds.shape[0]
    patch_count = own_patches.shape[0]
    work_count = slot_count // 2
    tile_count = lax.axis_size("tile")
    per_peer = (slot_count + tile_count - 1) // tile_count
    lane_total = tile_count * per_peer
    slot_alive = targets >= 0
    firsts = jnp.take(own_patches, first_index, axis=0)
    partners = jnp.concatenate([from_below, from_next], axis=0)
    seconds = jnp.take(partners, pair_kinds * patch_count + second_index, axis=0)
    pair_stack = jnp.stack([firsts, seconds], axis=1)
    slot_order = jnp.arange(slot_count, dtype=jnp.int32)
    earlier = (
        (targets[:, None] == targets[None, :])
        & (slot_order[None, :] < slot_order[:, None])
        & slot_alive[None, :]
    )
    position = jnp.sum(earlier.astype(jnp.int32), axis=1)
    lane_of_slot = jnp.where(slot_alive, targets * per_peer + position, -1)
    lane_ids = jnp.arange(lane_total, dtype=jnp.int32)
    lane_hits = lane_of_slot[None, :] == lane_ids[:, None]
    lane_used = jnp.any(lane_hits, axis=1)
    lane_source = jnp.sum(jnp.where(lane_hits, slot_order[None, :], 0), axis=1)
    lane_place = jnp.where(lane_used, jnp.take(places, lane_source), -1)
    work_ids = jnp.arange(work_count, dtype=jnp.int32)
    outgoing = jnp.take(pair_stack, lane_source, axis=0)
    arrived, arrived_place = (
        lax.all_to_all(outgoing, "tile", split_axis=0, concat_axis=0, tiled=True),
        lax.all_to_all(lane_place, "tile", split_axis=0, concat_axis=0, tiled=True),
    )
    present, picked = settle(arrived_place, lane_ids, work_ids)
    picks = jnp.stack([picked, picked, present.astype(jnp.int32)])
    surfaces, work_peaks = correlate_all(picks, arrived, arrived, 0, 1)
    returned = jnp.take(work_peaks, jnp.maximum(arrived_place, 0))
    returned = jnp.where(arrived_place >= 0, returned, jnp.zeros_like(returned))
    homecoming = lax.all_to_all(returned, "tile", split_axis=0, concat_axis=0, tiled=True)
    slot_peaks = jnp.take(homecoming, jnp.maximum(lane_of_slot, 0))
    peak_values = jnp.where(slot_alive, slot_peaks, jnp.zeros_like(slot_peaks))
    return (surfaces[None, None], peak_values[None, None])


def solution(mesh):
    in_specs = (
        P(("groups", "sect"), "tile", "half", None, None),
        P(None, ("groups", "sect"), "tile", "half"),
        P(None, ("groups", "sect"), "tile", "half"),
    )
    out_specs = (
        P(("groups", "sect"), "tile", "half", None, None),
        P(("groups", "sect"), "tile", "half"),
    )
    return jax.shard_map(body, mesh=mesh, in_specs=in_specs, out_specs=out_specs, check_vma=False)
```

```python
import functools

import jax
import jax.numpy as jnp
import numpy as np
from jax import lax
from jax.experimental import pallas as pl
from jax.experimental.pallas import tpu as pltpu
from jax.sharding import PartitionSpec as P

FLOOR = 0.05
STEPS = 32767.0
SMALLEST = 1.2e-34
MESH = pl.DeviceIdType.MESH


def real_tables(length):
    half = length // 2
    spots = np.arange(length)
    waves = np.arange(half)
    angles = (spots[:, None] * waves[None, :] % length) * (2.0 * np.pi / length)
    sines = np.sin(angles)
    sines[:, 0] = np.cos(np.pi * spots)
    table = np.concatenate([np.cos(angles), sines], axis=1).astype(np.float32)
    upper = table.astype(jnp.bfloat16)
    lower = (table - upper.astype(np.float32)).astype(jnp.bfloat16)
    column = np.stack([upper, lower])
    row = np.stack([upper.T, lower.T])
    return jnp.asarray(column), jnp.asarray(row)


def halves_of(value):
    upper = value.astype(jnp.bfloat16)
    return upper, (value - upper.astype(jnp.float32)).astype(jnp.bfloat16)


def dot(left, right):
    return jnp.dot(left, right, preferred_element_type=jnp.float32)


def left_product(table_ref, value):
    upper, lower = halves_of(value)
    return dot(table_ref[0], upper) + dot(table_ref[0], lower) + dot(table_ref[1], upper)


def right_product(value, table_ref):
    upper, lower = halves_of(value)
    return dot(upper, table_ref[0]) + dot(lower, table_ref[0]) + dot(upper, table_ref[1])


def packed_spectrum(picture, column_ref, row_ref):
    across = dot(picture, column_ref[0]) + dot(picture, column_ref[1])
    return left_product(row_ref, across)


def unpacked(packed, on_row, on_column):
    half = packed.shape[0] // 2
    cc, cs = packed[:half, :half], packed[:half, half:]
    sc, ss = packed[half:, :half], packed[half:, half:]
    edge = on_row | on_column
    plus_re = jnp.where(edge, cc, cc - ss)
    plus_im = jnp.where(on_row, cs, jnp.where(on_column, sc, sc + cs))
    minus_re = jnp.where(on_row, sc, jnp.where(on_column, cs, cc + ss))
    minus_im = jnp.where(edge, ss, cs - sc)
    return (plus_re, plus_im, minus_re, minus_im)


def phases(first_re, first_im, second_re, second_im, floor):
    cross_re = first_re * second_re + first_im * second_im
    cross_im = first_re * second_im - first_im * second_re
    power = cross_re * cross_re + cross_im * cross_im
    factor = jnp.minimum(lax.rsqrt(power), 1.0 / floor)
    return (cross_re * factor, cross_im * factor)


def correlate(first, second, column_ref, row_ref):
    length = first.shape[-1]
    half = length // 2
    floor = FLOOR * length * length
    first_packed = packed_spectrum(first, column_ref, row_ref)
    second_packed = packed_spectrum(second, column_ref, row_ref)
    rows = lax.broadcasted_iota(jnp.int32, (half, half), 0)
    columns = lax.broadcasted_iota(jnp.int32, (half, half), 1)
    on_row, on_column = rows == 0, columns == 0
    corner = on_row & on_column
    one = unpacked(first_packed, on_row, on_column)
    two = unpacked(second_packed, on_row, on_column)
    plus_re, plus_im = phases(one[0], one[1], two[0], two[1], floor)
    minus_re, minus_im = phases(one[2], one[3], two[2], two[3], floor)
    cc = jnp.where(on_row | on_column, plus_re, plus_re + minus_re)
    ss = jnp.where(on_row | on_column, -minus_im, minus_re - plus_re)
    sc = jnp.where(on_row, minus_re, jnp.where(on_column, -plus_im, minus_im - plus_im))
    cs = jnp.where(on_row, -plus_im, jnp.where(on_column, minus_re, -plus_im - minus_im))

    def at_corner(value, top, left):
        product = (
            first_packed[top : top + half, left : left + half]
            * second_packed[top : top + half, left : left + half]
        )
        real = product / jnp.maximum(jnp.abs(product), floor)
        return jnp.where(corner, 0.5 * real, value)

    packed = jnp.concatenate(
        [
            jnp.concatenate([at_corner(cc, 0, 0), at_corner(cs, 0, half)], axis=1),
            jnp.concatenate([at_corner(sc, half, 0), at_corner(ss, half, half)], axis=1),
        ],
        axis=0,
    )
    scale = 2.0 / length
    return left_product(column_ref, right_product(packed * scale, row_ref))


def rows_of(lists_ref, plan_ref, slots, target, position):
    def look(slot, carried):
        seen, chosen, used = carried
        hit = (plan_ref[0, 0, 0, slot] == target).astype(jnp.int32)
        match = hit * (seen == position).astype(jnp.int32)
        return (seen + hit, chosen + match * slot, used + match)

    zero = jnp.int32(0)
    _, chosen, used = lax.fori_loop(0, slots, look, (zero, zero, zero), unroll=True)
    return chosen, used


def stitch_kernel(
    sizes,
    lists_ref,
    plan_ref,
    own_ref,
    column_ref,
    row_ref,
    surface_ref,
    peak_ref,
    below_ref,
    next_ref,
    sent_ref,
    sent_note_ref,
    got_ref,
    got_note_ref,
    fetch_send,
    fetch_recv,
    code_send,
    code_recv,
    note_send,
    note_recv,
):
    tiles, sections, per_peer, slots, works = sizes
    tile, sect = lax.axis_index("tile"), lax.axis_index("sect")
    lanes = tiles * per_peer

    barrier = pltpu.get_barrier_semaphore()
    for shift in range(1, tiles):
        pl.semaphore_signal(
            barrier, inc=1, device_id={"tile": lax.rem(tile + shift, tiles)}, device_id_type=MESH
        )

    @pl.when(sect > 0)
    def _():
        pl.semaphore_signal(barrier, inc=1, device_id={"sect": sect - 1}, device_id_type=MESH)

    @pl.when(sect < sections - 1)
    def _():
        pl.semaphore_signal(barrier, inc=1, device_id={"sect": sect + 1}, device_id_type=MESH)

    neighbours = lax.min(sect, 1) + lax.min(sections - 1 - sect, 1)
    pl.semaphore_wait(barrier, tiles - 1 + neighbours)

    def fetch(axis, place, target_ref, index):
        return pltpu.make_async_remote_copy(
            src_ref=own_ref.at[0, 0],
            dst_ref=target_ref,
            send_sem=fetch_send.at[index],
            recv_sem=fetch_recv.at[index],
            device_id={axis: place},
            device_id_type=MESH,
        )

    to_above = fetch("tile", lax.max(tile - 1, 0), below_ref, 0)
    to_before = fetch("sect", lax.max(sect - 1, 0), next_ref, 1)

    @pl.when(tile > 0)
    def _():
        to_above.start()

    @pl.when(sect > 0)
    def _():
        to_before.start()

    surface_ref[...] = jnp.zeros_like(surface_ref)
    peak_ref[...] = jnp.zeros_like(peak_ref)

    @pl.when(tile < tiles - 1)
    def _():
        to_above.wait_recv()

    @pl.when(sect < sections - 1)
    def _():
        to_before.wait_recv()

    def copies(lane, target):
        code = pltpu.make_async_remote_copy(
            src_ref=sent_ref.at[lane],
            dst_ref=got_ref.at[lane],
            send_sem=code_send.at[lane],
            recv_sem=code_recv.at[lane],
            device_id={"tile": target},
            device_id_type=MESH,
        )
        note = pltpu.make_async_remote_copy(
            src_ref=sent_note_ref.at[lane],
            dst_ref=got_note_ref.at[lane],
            send_sem=note_send.at[lane],
            recv_sem=note_recv.at[lane],
            device_id={"tile": target},
            device_id_type=MESH,
        )
        return code, note

    slot_ids = lax.broadcasted_iota(jnp.int32, peak_ref.shape, 1)

    def settle(code, note):
        found = code.astype(jnp.int32).astype(jnp.float32) * note[0:1]
        place = note[1:2]
        for work in range(works):
            surface_ref[0, 0, work] = jnp.where(
                place == float(work), found, surface_ref[0, 0, work]
            )

    def correlate_lane(lane, carried):
        shift = tiles - 1 - lane // per_peer
        target = lax.rem(tile + shift, tiles)
        slot, used = rows_of(lists_ref, plan_ref, slots, target, lax.rem(lane, per_peer))
        kind = lists_ref[0, 0, 0, slot]
        first = own_ref[0, 0, lists_ref[1, 0, 0, slot]]
        other = lists_ref[2, 0, 0, slot]
        second = jnp.where(kind == 0, below_ref[other], next_ref[other])
        surface = correlate(first, second, column_ref, row_ref)
        peak = jnp.max(surface)
        peak_ref[...] = jnp.where(
            (slot_ids == slot) & (used > 0), jnp.full(peak_ref.shape, peak), peak_ref[...]
        )
        place = jnp.where(used > 0, plan_ref[1, 0, 0, slot], -1).astype(jnp.float32)
        tallest = jnp.max(jnp.abs(surface), axis=0, keepdims=True)
        tallest = jnp.maximum(tallest, SMALLEST)
        code = jnp.round(surface * (STEPS / tallest)).astype(jnp.int32).astype(jnp.int16)
        sent_ref[lane] = code
        note_row = lax.broadcasted_iota(jnp.int32, sent_note_ref.shape[1:], 0)
        sent_note_ref[lane] = jnp.where(note_row == 0, tallest * (1.0 / STEPS), place)

        @pl.when(shift > 0)
        def _():
            code_copy, note_copy = copies(lane, target)
            note_copy.start()
            code_copy.start()

        return carried

    lax.fori_loop(0, lanes, correlate_lane, 0)

    def settle_own(lane, carried):
        settle(sent_ref[lane], sent_note_ref[lane])
        return carried

    lax.fori_loop(lanes - per_peer, lanes, settle_own, 0)

    def settle_lane(lane, carried):
        code_copy, note_copy = copies(lane, lax.rem(tile + tiles - 1 - lane // per_peer, tiles))
        note_copy.wait()
        code_copy.wait()
        settle(got_ref[lane], got_note_ref[lane])
        return carried

    lax.fori_loop(0, lanes - per_peer, settle_lane, 0)

    @pl.when(tile > 0)
    def _():
        to_above.wait_send()

    @pl.when(sect > 0)
    def _():
        to_before.wait_send()


def body(patches, pair_lists, move_plan):
    length = patches.shape[-1]
    slots = pair_lists.shape[-1]
    works = slots // 2
    tiles, sections = lax.axis_size("tile"), lax.axis_size("sect")
    per_peer = (slots + tiles - 1) // tiles
    lanes = tiles * per_peer
    column, row = real_tables(length)
    vmem = pl.BlockSpec(memory_space=pltpu.VMEM)
    smem = pl.BlockSpec(memory_space=pltpu.SMEM)
    surfaces, peaks = pl.pallas_call(
        functools.partial(stitch_kernel, (tiles, sections, per_peer, slots, works)),
        in_specs=[smem, smem, vmem, vmem, vmem],
        out_specs=[vmem, vmem],
        out_shape=[
            jax.ShapeDtypeStruct((1, 1, works, length, length), jnp.float32),
            jax.ShapeDtypeStruct((1, 128), jnp.float32),
        ],
        scratch_shapes=[
            pltpu.VMEM(patches.shape[2:], jnp.bfloat16),
            pltpu.VMEM(patches.shape[2:], jnp.bfloat16),
            pltpu.VMEM((lanes, length, length), jnp.int16),
            pltpu.VMEM((lanes, 8, length), jnp.float32),
            pltpu.VMEM((lanes, length, length), jnp.int16),
            pltpu.VMEM((lanes, 8, length), jnp.float32),
            pltpu.SemaphoreType.DMA((2,)),
            pltpu.SemaphoreType.DMA((2,)),
            pltpu.SemaphoreType.DMA((lanes,)),
            pltpu.SemaphoreType.DMA((lanes,)),
            pltpu.SemaphoreType.DMA((lanes,)),
            pltpu.SemaphoreType.DMA((lanes,)),
        ],
        compiler_params=pltpu.CompilerParams(collective_id=0, has_side_effects=True),
    )(pair_lists, move_plan, patches, column, row)
    return (surfaces, peaks[:, None, :slots])


def solution(mesh):
    in_specs = (
        P(("groups", "sect"), "tile", "half", None, None),
        P(None, ("groups", "sect"), "tile", "half"),
        P(None, ("groups", "sect"), "tile", "half"),
    )
    out_specs = (
        P(("groups", "sect"), "tile", "half", None, None),
        P(("groups", "sect"), "tile", "half"),
    )
    return jax.shard_map(body, mesh=mesh, in_specs=in_specs, out_specs=out_specs, check_vma=False)
```

```python
import functools

import jax
import jax.numpy as jnp
import numpy as np
from jax import lax
from jax.experimental import pallas as pl
from jax.experimental.pallas import tpu as pltpu
from jax.sharding import PartitionSpec as P

FLOOR = 0.05
STEPS = 32767.0
SMALLEST = 1.2e-34
MESH = pl.DeviceIdType.MESH


def real_tables(length):
    half = length // 2
    spots = np.arange(length)
    waves = np.arange(half)
    angles = (spots[:, None] * waves[None, :] % length) * (2.0 * np.pi / length)
    sines = np.sin(angles)
    sines[:, 0] = np.cos(np.pi * spots)
    table = np.concatenate([np.cos(angles), sines], axis=1).astype(np.float32)
    upper = table.astype(jnp.bfloat16)
    lower = (table - upper.astype(np.float32)).astype(jnp.bfloat16)
    column = np.stack([upper, lower])
    row = np.stack([upper.T, lower.T])
    return jnp.asarray(column), jnp.asarray(row)


def halves_of(value):
    upper = value.astype(jnp.bfloat16)
    return upper, (value - upper.astype(jnp.float32)).astype(jnp.bfloat16)


def dot(left, right):
    return jnp.dot(left, right, preferred_element_type=jnp.float32)


def left_product(table_ref, value):
    upper, lower = halves_of(value)
    return dot(table_ref[0], upper) + dot(table_ref[0], lower) + dot(table_ref[1], upper)


def right_product(value, table_ref):
    upper, lower = halves_of(value)
    return dot(upper, table_ref[0]) + dot(lower, table_ref[0]) + dot(upper, table_ref[1])


def packed_spectrum(picture, column_ref, row_ref):
    across = dot(picture, column_ref[0]) + dot(picture, column_ref[1])
    return left_product(row_ref, across)


def unpacked(packed, on_row, on_column):
    half = packed.shape[0] // 2
    cc, cs = packed[:half, :half], packed[:half, half:]
    sc, ss = packed[half:, :half], packed[half:, half:]
    edge = on_row | on_column
    plus_re = jnp.where(edge, cc, cc - ss)
    plus_im = jnp.where(on_row, cs, jnp.where(on_column, sc, sc + cs))
    minus_re = jnp.where(on_row, sc, jnp.where(on_column, cs, cc + ss))
    minus_im = jnp.where(edge, ss, cs - sc)
    return (plus_re, plus_im, minus_re, minus_im)


def phases(first_re, first_im, second_re, second_im, floor):
    cross_re = first_re * second_re + first_im * second_im
    cross_im = first_re * second_im - first_im * second_re
    power = cross_re * cross_re + cross_im * cross_im
    factor = jnp.minimum(lax.rsqrt(power), 1.0 / floor)
    return (cross_re * factor, cross_im * factor)


def correlate(first, second, column_ref, row_ref):
    length = first.shape[-1]
    half = length // 2
    floor = FLOOR * length * length
    first_packed = packed_spectrum(first, column_ref, row_ref)
    second_packed = packed_spectrum(second, column_ref, row_ref)
    rows = lax.broadcasted_iota(jnp.int32, (half, half), 0)
    columns = lax.broadcasted_iota(jnp.int32, (half, half), 1)
    on_row, on_column = rows == 0, columns == 0
    corner = on_row & on_column
    one = unpacked(first_packed, on_row, on_column)
    two = unpacked(second_packed, on_row, on_column)
    plus_re, plus_im = phases(one[0], one[1], two[0], two[1], floor)
    minus_re, minus_im = phases(one[2], one[3], two[2], two[3], floor)
    cc = jnp.where(on_row | on_column, plus_re, plus_re + minus_re)
    ss = jnp.where(on_row | on_column, -minus_im, minus_re - plus_re)
    sc = jnp.where(on_row, minus_re, jnp.where(on_column, -plus_im, minus_im - plus_im))
    cs = jnp.where(on_row, -plus_im, jnp.where(on_column, minus_re, -plus_im - minus_im))

    def at_corner(value, top, left):
        product = (
            first_packed[top : top + half, left : left + half]
            * second_packed[top : top + half, left : left + half]
        )
        real = product / jnp.maximum(jnp.abs(product), floor)
        return jnp.where(corner, 0.5 * real, value)

    packed = jnp.concatenate(
        [
            jnp.concatenate([at_corner(cc, 0, 0), at_corner(cs, 0, half)], axis=1),
            jnp.concatenate([at_corner(sc, half, 0), at_corner(ss, half, half)], axis=1),
        ],
        axis=0,
    )
    scale = 2.0 / length
    return left_product(column_ref, right_product(packed * scale, row_ref))


def passed_on(value, axis):
    count = lax.axis_size(axis)
    return lax.ppermute(value, axis, [(source, source + 1) for source in range(count - 1)])


def slot_of(table_ref, target, position):
    def look(slot, carried):
        seen, chosen, used = carried
        hit = (table_ref[3, 0, 0, slot] == target).astype(jnp.int32)
        match = hit * (seen == position).astype(jnp.int32)
        return (seen + hit, chosen + match * slot, used + match)

    zero = jnp.int32(0)
    slots = table_ref.shape[-1]
    _, chosen, used = lax.fori_loop(0, slots, look, (zero, zero, zero), unroll=True)
    return chosen, used


def stitch_kernel(
    sizes,
    table_ref,
    above_table_ref,
    before_table_ref,
    own_ref,
    column_ref,
    row_ref,
    surface_ref,
    peak_ref,
    to_above_ref,
    to_before_ref,
    below_ref,
    next_ref,
    sent_ref,
    sent_note_ref,
    got_ref,
    got_note_ref,
    fetch_send,
    fetch_recv,
    code_send,
    code_recv,
    note_send,
    note_recv,
):
    tiles, sections, per_peer, works = sizes
    tile, sect = lax.axis_index("tile"), lax.axis_index("sect")
    lanes = tiles * per_peer

    barrier = pltpu.get_barrier_semaphore()
    for shift in range(1, tiles):
        pl.semaphore_signal(
            barrier, inc=1, device_id={"tile": lax.rem(tile + shift, tiles)}, device_id_type=MESH
        )

    @pl.when(sect > 0)
    def _():
        pl.semaphore_signal(barrier, inc=1, device_id={"sect": sect - 1}, device_id_type=MESH)

    @pl.when(sect < sections - 1)
    def _():
        pl.semaphore_signal(barrier, inc=1, device_id={"sect": sect + 1}, device_id_type=MESH)

    neighbours = lax.min(sect, 1) + lax.min(sections - 1 - sect, 1)
    pl.semaphore_wait(barrier, tiles - 1 + neighbours)

    def target_of(owner_tile, lane):
        return lax.rem(owner_tile + tiles - 1 - lane // per_peer, tiles)

    def stage(lane, carried):
        position = lax.rem(lane, per_peer)
        slot, _ = slot_of(above_table_ref, target_of(tile + tiles - 1, lane), position)
        to_above_ref[lane] = own_ref[0, 0, above_table_ref[2, 0, 0, slot]]
        slot, _ = slot_of(before_table_ref, target_of(tile, lane), position)
        to_before_ref[lane] = own_ref[0, 0, before_table_ref[2, 0, 0, slot]]
        return carried

    lax.fori_loop(0, lanes, stage, 0)

    def to_above(lane):
        return pltpu.make_async_remote_copy(
            src_ref=to_above_ref.at[lane],
            dst_ref=below_ref.at[lane],
            send_sem=fetch_send.at[0, lane],
            recv_sem=fetch_recv.at[0, lane],
            device_id={"tile": lax.max(tile - 1, 0)},
            device_id_type=MESH,
        )

    def to_before(lane):
        return pltpu.make_async_remote_copy(
            src_ref=to_before_ref.at[lane],
            dst_ref=next_ref.at[lane],
            send_sem=fetch_send.at[1, lane],
            recv_sem=fetch_recv.at[1, lane],
            device_id={"sect": lax.max(sect - 1, 0)},
            device_id_type=MESH,
        )

    def send_patches(lane, carried):
        @pl.when(tile > 0)
        def _():
            to_above(lane).start()

        @pl.when(sect > 0)
        def _():
            to_before(lane).start()

        return carried

    lax.fori_loop(0, lanes, send_patches, 0)
    surface_ref[...] = jnp.zeros_like(surface_ref)
    peak_ref[...] = jnp.zeros_like(peak_ref)

    def copies(lane, target):
        code = pltpu.make_async_remote_copy(
            src_ref=sent_ref.at[lane],
            dst_ref=got_ref.at[lane],
            send_sem=code_send.at[lane],
            recv_sem=code_recv.at[lane],
            device_id={"tile": target},
            device_id_type=MESH,
        )
        note = pltpu.make_async_remote_copy(
            src_ref=sent_note_ref.at[lane],
            dst_ref=got_note_ref.at[lane],
            send_sem=note_send.at[lane],
            recv_sem=note_recv.at[lane],
            device_id={"tile": target},
            device_id_type=MESH,
        )
        return code, note

    slot_ids = lax.broadcasted_iota(jnp.int32, peak_ref.shape, 1)

    def settle(code, note):
        found = code.astype(jnp.int32).astype(jnp.float32) * note[0:1]
        place = note[1:2]
        for work in range(works):
            surface_ref[0, 0, work] = jnp.where(
                place == float(work), found, surface_ref[0, 0, work]
            )

    def correlate_lane(lane, carried):
        shift = tiles - 1 - lane // per_peer
        target = target_of(tile, lane)
        slot, used = slot_of(table_ref, target, lax.rem(lane, per_peer))
        kind = table_ref[0, 0, 0, slot]
        first = own_ref[0, 0, table_ref[1, 0, 0, slot]]

        @pl.when(tile < tiles - 1)
        def _():
            to_above(lane).wait_recv()

        @pl.when(sect < sections - 1)
        def _():
            to_before(lane).wait_recv()

        second = jnp.where(kind == 0, below_ref[lane], next_ref[lane])
        surface = correlate(first, second, column_ref, row_ref)
        peak = jnp.max(surface)
        peak_ref[...] = jnp.where(
            (slot_ids == slot) & (used > 0), jnp.full(peak_ref.shape, peak), peak_ref[...]
        )
        place = jnp.where(used > 0, table_ref[4, 0, 0, slot], -1).astype(jnp.float32)
        tallest = jnp.max(jnp.abs(surface), axis=0, keepdims=True)
        tallest = jnp.maximum(tallest, SMALLEST)
        code = jnp.round(surface * (STEPS / tallest)).astype(jnp.int32).astype(jnp.int16)
        sent_ref[lane] = code
        note_row = lax.broadcasted_iota(jnp.int32, sent_note_ref.shape[1:], 0)
        sent_note_ref[lane] = jnp.where(note_row == 0, tallest * (1.0 / STEPS), place)

        @pl.when(shift > 0)
        def _():
            code_copy, note_copy = copies(lane, target)
            note_copy.start()
            code_copy.start()

        return carried

    lax.fori_loop(0, lanes, correlate_lane, 0)

    def settle_own(lane, carried):
        settle(sent_ref[lane], sent_note_ref[lane])
        return carried

    lax.fori_loop(lanes - per_peer, lanes, settle_own, 0)

    def settle_lane(lane, carried):
        code_copy, note_copy = copies(lane, target_of(tile, lane))
        note_copy.wait()
        code_copy.wait()
        settle(got_ref[lane], got_note_ref[lane])
        return carried

    lax.fori_loop(0, lanes - per_peer, settle_lane, 0)

    def patches_left(lane, carried):
        @pl.when(tile > 0)
        def _():
            to_above(lane).wait_send()

        @pl.when(sect > 0)
        def _():
            to_before(lane).wait_send()

        return carried

    lax.fori_loop(0, lanes, patches_left, 0)


def body(patches, pair_lists, move_plan):
    length = patches.shape[-1]
    slots = pair_lists.shape[-1]
    works = slots // 2
    tiles, sections = lax.axis_size("tile"), lax.axis_size("sect")
    per_peer = (slots + tiles - 1) // tiles
    lanes = tiles * per_peer
    column, row = real_tables(length)
    table = jnp.concatenate([pair_lists, move_plan], axis=0)
    above_table, before_table = passed_on(table, "tile"), passed_on(table, "sect")
    vmem = pl.BlockSpec(memory_space=pltpu.VMEM)
    smem = pl.BlockSpec(memory_space=pltpu.SMEM)
    surfaces, peaks = pl.pallas_call(
        functools.partial(stitch_kernel, (tiles, sections, per_peer, works)),
        in_specs=[smem, smem, smem, vmem, vmem, vmem],
        out_specs=[vmem, vmem],
        out_shape=[
            jax.ShapeDtypeStruct((1, 1, works, length, length), jnp.float32),
            jax.ShapeDtypeStruct((1, 128), jnp.float32),
        ],
        scratch_shapes=[
            pltpu.VMEM((lanes, length, length), jnp.bfloat16),
            pltpu.VMEM((lanes, length, length), jnp.bfloat16),
            pltpu.VMEM((lanes, length, length), jnp.bfloat16),
            pltpu.VMEM((lanes, length, length), jnp.bfloat16),
            pltpu.VMEM((lanes, length, length), jnp.int16),
            pltpu.VMEM((lanes, 8, length), jnp.float32),
            pltpu.VMEM((lanes, length, length), jnp.int16),
            pltpu.VMEM((lanes, 8, length), jnp.float32),
            pltpu.SemaphoreType.DMA((2, lanes)),
            pltpu.SemaphoreType.DMA((2, lanes)),
            pltpu.SemaphoreType.DMA((lanes,)),
            pltpu.SemaphoreType.DMA((lanes,)),
            pltpu.SemaphoreType.DMA((lanes,)),
            pltpu.SemaphoreType.DMA((lanes,)),
        ],
        compiler_params=pltpu.CompilerParams(collective_id=0, has_side_effects=True),
    )(table, above_table, before_table, patches, column, row)
    return (surfaces, peaks[:, None, :slots])


def solution(mesh):
    in_specs = (
        P(("groups", "sect"), "tile", "half", None, None),
        P(None, ("groups", "sect"), "tile", "half"),
        P(None, ("groups", "sect"), "tile", "half"),
    )
    out_specs = (
        P(("groups", "sect"), "tile", "half", None, None),
        P(("groups", "sect"), "tile", "half"),
    )
    return jax.shard_map(body, mesh=mesh, in_specs=in_specs, out_specs=out_specs, check_vma=False)
```

```python
import functools

import jax
import jax.numpy as jnp
import numpy as np
from jax import lax
from jax.experimental import pallas as pl
from jax.experimental.pallas import tpu as pltpu
from jax.sharding import PartitionSpec as P

FLOOR = 0.05
STEPS = 32767.0
SMALLEST = 1.2e-34
MESH = pl.DeviceIdType.MESH


def real_tables(length):
    half = length // 2
    spots = np.arange(length)
    waves = np.arange(half)
    angles = (spots[:, None] * waves[None, :] % length) * (2.0 * np.pi / length)
    sines = np.sin(angles)
    sines[:, 0] = np.cos(np.pi * spots)
    table = np.concatenate([np.cos(angles), sines], axis=1).astype(np.float32)
    upper = table.astype(jnp.bfloat16)
    lower = (table - upper.astype(np.float32)).astype(jnp.bfloat16)
    column = np.stack([upper, lower])
    row = np.stack([upper.T, lower.T])
    return jnp.asarray(column), jnp.asarray(row)


def halves_of(value):
    upper = value.astype(jnp.bfloat16)
    return upper, (value - upper.astype(jnp.float32)).astype(jnp.bfloat16)


def dot(left, right):
    return jnp.dot(left, right, preferred_element_type=jnp.float32)


def left_product(table_ref, value):
    upper, lower = halves_of(value)
    return dot(table_ref[0], upper) + dot(table_ref[0], lower) + dot(table_ref[1], upper)


def right_product(value, table_ref):
    upper, lower = halves_of(value)
    return dot(upper, table_ref[0]) + dot(lower, table_ref[0]) + dot(upper, table_ref[1])


def packed_spectrum(picture, column_ref, row_ref):
    across = dot(picture, column_ref[0]) + dot(picture, column_ref[1])
    return left_product(row_ref, across)


def unpacked(packed, on_row, on_column):
    half = packed.shape[0] // 2
    cc, cs = packed[:half, :half], packed[:half, half:]
    sc, ss = packed[half:, :half], packed[half:, half:]
    edge = on_row | on_column
    plus_re = jnp.where(edge, cc, cc - ss)
    plus_im = jnp.where(on_row, cs, jnp.where(on_column, sc, sc + cs))
    minus_re = jnp.where(on_row, sc, jnp.where(on_column, cs, cc + ss))
    minus_im = jnp.where(edge, ss, cs - sc)
    return (plus_re, plus_im, minus_re, minus_im)


def phases(first_re, first_im, second_re, second_im, floor):
    cross_re = first_re * second_re + first_im * second_im
    cross_im = first_re * second_im - first_im * second_re
    power = cross_re * cross_re + cross_im * cross_im
    factor = jnp.minimum(lax.rsqrt(power), 1.0 / floor)
    return (cross_re * factor, cross_im * factor)


def correlate(first, second, column_ref, row_ref):
    length = first.shape[-1]
    half = length // 2
    floor = FLOOR * length * length
    first_packed = packed_spectrum(first, column_ref, row_ref)
    second_packed = packed_spectrum(second, column_ref, row_ref)
    rows = lax.broadcasted_iota(jnp.int32, (half, half), 0)
    columns = lax.broadcasted_iota(jnp.int32, (half, half), 1)
    on_row, on_column = rows == 0, columns == 0
    corner = on_row & on_column
    one = unpacked(first_packed, on_row, on_column)
    two = unpacked(second_packed, on_row, on_column)
    plus_re, plus_im = phases(one[0], one[1], two[0], two[1], floor)
    minus_re, minus_im = phases(one[2], one[3], two[2], two[3], floor)
    cc = jnp.where(on_row | on_column, plus_re, plus_re + minus_re)
    ss = jnp.where(on_row | on_column, -minus_im, minus_re - plus_re)
    sc = jnp.where(on_row, minus_re, jnp.where(on_column, -plus_im, minus_im - plus_im))
    cs = jnp.where(on_row, -plus_im, jnp.where(on_column, minus_re, -plus_im - minus_im))

    def at_corner(value, top, left):
        product = (
            first_packed[top : top + half, left : left + half]
            * second_packed[top : top + half, left : left + half]
        )
        real = product / jnp.maximum(jnp.abs(product), floor)
        return jnp.where(corner, 0.5 * real, value)

    packed = jnp.concatenate(
        [
            jnp.concatenate([at_corner(cc, 0, 0), at_corner(cs, 0, half)], axis=1),
            jnp.concatenate([at_corner(sc, half, 0), at_corner(ss, half, half)], axis=1),
        ],
        axis=0,
    )
    scale = 2.0 / length
    return left_product(column_ref, right_product(packed * scale, row_ref))


def slot_of(plan_ref, target, position):
    def look(slot, carried):
        seen, chosen, used = carried
        hit = (plan_ref[0, 0, 0, slot] == target).astype(jnp.int32)
        match = hit * (seen == position).astype(jnp.int32)
        return (seen + hit, chosen + match * slot, used + match)

    zero = jnp.int32(0)
    slots = plan_ref.shape[-1]
    _, chosen, used = lax.fori_loop(0, slots, look, (zero, zero, zero), unroll=True)
    return chosen, used


def stitch_kernel(
    sizes,
    lists_ref,
    plan_ref,
    patches_ref,
    column_ref,
    row_ref,
    surface_ref,
    peak_ref,
    own_ref,
    above_lists_ref,
    above_plan_ref,
    before_lists_ref,
    before_plan_ref,
    to_above_ref,
    to_before_ref,
    below_ref,
    next_ref,
    sent_ref,
    sent_note_ref,
    got_ref,
    got_note_ref,
    load_sem,
    list_send,
    list_recv,
    fetch_send,
    fetch_recv,
    code_send,
    code_recv,
    note_send,
    note_recv,
):
    tiles, sections, per_peer, works = sizes
    tile, sect = lax.axis_index("tile"), lax.axis_index("sect")
    lanes = tiles * per_peer

    load = pltpu.make_async_copy(patches_ref.at[0, 0], own_ref, load_sem)
    load.start()
    barrier = pltpu.get_barrier_semaphore()
    for shift in range(1, tiles):
        pl.semaphore_signal(
            barrier, inc=1, device_id={"tile": lax.rem(tile + shift, tiles)}, device_id_type=MESH
        )

    @pl.when(sect > 0)
    def _():
        pl.semaphore_signal(barrier, inc=1, device_id={"sect": sect - 1}, device_id_type=MESH)

    @pl.when(sect < sections - 1)
    def _():
        pl.semaphore_signal(barrier, inc=1, device_id={"sect": sect + 1}, device_id_type=MESH)

    neighbours = lax.min(sect, 1) + lax.min(sections - 1 - sect, 1)
    pl.semaphore_wait(barrier, tiles - 1 + neighbours)

    def list_copies(axis, place, refs, first_sem):
        return [
            pltpu.make_async_remote_copy(
                src_ref=source,
                dst_ref=target,
                send_sem=list_send.at[first_sem + index],
                recv_sem=list_recv.at[first_sem + index],
                device_id={axis: place},
                device_id_type=MESH,
            )
            for index, (source, target) in enumerate(zip((lists_ref, plan_ref), refs))
        ]

    to_below = list_copies(
        "tile", lax.min(tile + 1, tiles - 1), (above_lists_ref, above_plan_ref), 0
    )
    to_next = list_copies(
        "sect", lax.min(sect + 1, sections - 1), (before_lists_ref, before_plan_ref), 2
    )

    @pl.when(tile < tiles - 1)
    def _():
        for copy in to_below:
            copy.start()

    @pl.when(sect < sections - 1)
    def _():
        for copy in to_next:
            copy.start()

    surface_ref[...] = jnp.zeros_like(surface_ref)
    peak_ref[...] = jnp.zeros_like(peak_ref)
    load.wait()

    def target_of(owner_tile, lane):
        return lax.rem(owner_tile + tiles - 1 - lane // per_peer, tiles)

    def to_above(lane):
        return pltpu.make_async_remote_copy(
            src_ref=to_above_ref.at[lane],
            dst_ref=below_ref.at[lane],
            send_sem=fetch_send.at[0, lane],
            recv_sem=fetch_recv.at[0, lane],
            device_id={"tile": lax.max(tile - 1, 0)},
            device_id_type=MESH,
        )

    def to_before(lane):
        return pltpu.make_async_remote_copy(
            src_ref=to_before_ref.at[lane],
            dst_ref=next_ref.at[lane],
            send_sem=fetch_send.at[1, lane],
            recv_sem=fetch_recv.at[1, lane],
            device_id={"sect": lax.max(sect - 1, 0)},
            device_id_type=MESH,
        )

    @pl.when(tile > 0)
    def _():
        for copy in to_below:
            copy.wait_recv()

        def stage(lane, carried):
            slot, _ = slot_of(
                above_plan_ref, target_of(tile + tiles - 1, lane), lax.rem(lane, per_peer)
            )
            to_above_ref[lane] = own_ref[above_lists_ref[2, 0, 0, slot]]
            return carried

        lax.fori_loop(0, lanes, stage, 0)

        def send(lane, carried):
            to_above(lane).start()
            return carried

        lax.fori_loop(0, lanes, send, 0)

    @pl.when(sect > 0)
    def _():
        for copy in to_next:
            copy.wait_recv()

        def stage(lane, carried):
            slot, _ = slot_of(before_plan_ref, target_of(tile, lane), lax.rem(lane, per_peer))
            to_before_ref[lane] = own_ref[before_lists_ref[2, 0, 0, slot]]
            return carried

        lax.fori_loop(0, lanes, stage, 0)

        def send(lane, carried):
            to_before(lane).start()
            return carried

        lax.fori_loop(0, lanes, send, 0)

    def copies(lane, target):
        code = pltpu.make_async_remote_copy(
            src_ref=sent_ref.at[lane],
            dst_ref=got_ref.at[lane],
            send_sem=code_send.at[lane],
            recv_sem=code_recv.at[lane],
            device_id={"tile": target},
            device_id_type=MESH,
        )
        note = pltpu.make_async_remote_copy(
            src_ref=sent_note_ref.at[lane],
            dst_ref=got_note_ref.at[lane],
            send_sem=note_send.at[lane],
            recv_sem=note_recv.at[lane],
            device_id={"tile": target},
            device_id_type=MESH,
        )
        return code, note

    slot_ids = lax.broadcasted_iota(jnp.int32, peak_ref.shape, 2)

    def settle(code, note):
        found = code.astype(jnp.int32).astype(jnp.float32) * note[0:1]
        place = note[1:2]
        for work in range(works):
            surface_ref[0, 0, work] = jnp.where(
                place == float(work), found, surface_ref[0, 0, work]
            )

    def correlate_lane(lane, carried):
        shift = tiles - 1 - lane // per_peer
        target = target_of(tile, lane)
        slot, used = slot_of(plan_ref, target, lax.rem(lane, per_peer))
        kind = lists_ref[0, 0, 0, slot]
        first = own_ref[lists_ref[1, 0, 0, slot]]

        @pl.when(tile < tiles - 1)
        def _():
            to_above(lane).wait_recv()

        @pl.when(sect < sections - 1)
        def _():
            to_before(lane).wait_recv()

        second = jnp.where(kind == 0, below_ref[lane], next_ref[lane])
        surface = correlate(first, second, column_ref, row_ref)
        peak = jnp.max(surface)
        peak_ref[...] = jnp.where(
            (slot_ids == slot) & (used > 0), jnp.full(peak_ref.shape, peak), peak_ref[...]
        )
        place = jnp.where(used > 0, plan_ref[1, 0, 0, slot], -1).astype(jnp.float32)
        tallest = jnp.max(jnp.abs(surface), axis=0, keepdims=True)
        tallest = jnp.maximum(tallest, SMALLEST)
        code = jnp.round(surface * (STEPS / tallest)).astype(jnp.int32).astype(jnp.int16)
        sent_ref[lane] = code
        note_row = lax.broadcasted_iota(jnp.int32, sent_note_ref.shape[1:], 0)
        sent_note_ref[lane] = jnp.where(note_row == 0, tallest * (1.0 / STEPS), place)

        @pl.when(shift > 0)
        def _():
            code_copy, note_copy = copies(lane, target)
            note_copy.start()
            code_copy.start()

        return carried

    lax.fori_loop(0, lanes, correlate_lane, 0)

    def settle_own(lane, carried):
        settle(sent_ref[lane], sent_note_ref[lane])
        return carried

    lax.fori_loop(lanes - per_peer, lanes, settle_own, 0)

    def settle_lane(lane, carried):
        code_copy, note_copy = copies(lane, target_of(tile, lane))
        note_copy.wait()
        code_copy.wait()
        settle(got_ref[lane], got_note_ref[lane])
        return carried

    lax.fori_loop(0, lanes - per_peer, settle_lane, 0)

    def patches_left(lane, carried):
        @pl.when(tile > 0)
        def _():
            to_above(lane).wait_send()

        @pl.when(sect > 0)
        def _():
            to_before(lane).wait_send()

        return carried

    lax.fori_loop(0, lanes, patches_left, 0)

    @pl.when(tile < tiles - 1)
    def _():
        for copy in to_below:
            copy.wait_send()

    @pl.when(sect < sections - 1)
    def _():
        for copy in to_next:
            copy.wait_send()


def body(patches, pair_lists, move_plan):
    length = patches.shape[-1]
    slots = pair_lists.shape[-1]
    works = slots // 2
    tiles, sections = lax.axis_size("tile"), lax.axis_size("sect")
    per_peer = (slots + tiles - 1) // tiles
    lanes = tiles * per_peer
    column, row = real_tables(length)
    vmem = pl.BlockSpec(memory_space=pltpu.VMEM)
    smem = pl.BlockSpec(memory_space=pltpu.SMEM)
    surfaces, peaks = pl.pallas_call(
        functools.partial(stitch_kernel, (tiles, sections, per_peer, works)),
        in_specs=[smem, smem, pl.BlockSpec(memory_space=pl.ANY), vmem, vmem],
        out_specs=[vmem, vmem],
        out_shape=[
            jax.ShapeDtypeStruct((1, 1, works, length, length), jnp.float32),
            jax.ShapeDtypeStruct((1, 1, slots), jnp.float32),
        ],
        scratch_shapes=[
            pltpu.VMEM(patches.shape[2:], jnp.bfloat16),
            pltpu.SMEM(pair_lists.shape, jnp.int32),
            pltpu.SMEM(move_plan.shape, jnp.int32),
            pltpu.SMEM(pair_lists.shape, jnp.int32),
            pltpu.SMEM(move_plan.shape, jnp.int32),
            pltpu.VMEM((lanes, length, length), jnp.bfloat16),
            pltpu.VMEM((lanes, length, length), jnp.bfloat16),
            pltpu.VMEM((lanes, length, length), jnp.bfloat16),
            pltpu.VMEM((lanes, length, length), jnp.bfloat16),
            pltpu.VMEM((lanes, length, length), jnp.int16),
            pltpu.VMEM((lanes, 8, length), jnp.float32),
            pltpu.VMEM((lanes, length, length), jnp.int16),
            pltpu.VMEM((lanes, 8, length), jnp.float32),
            pltpu.SemaphoreType.DMA(()),
            pltpu.SemaphoreType.DMA((4,)),
            pltpu.SemaphoreType.DMA((4,)),
            pltpu.SemaphoreType.DMA((2, lanes)),
            pltpu.SemaphoreType.DMA((2, lanes)),
            pltpu.SemaphoreType.DMA((lanes,)),
            pltpu.SemaphoreType.DMA((lanes,)),
            pltpu.SemaphoreType.DMA((lanes,)),
            pltpu.SemaphoreType.DMA((lanes,)),
        ],
        compiler_params=pltpu.CompilerParams(collective_id=0, has_side_effects=True),
    )(pair_lists, move_plan, patches, column, row)
    return (surfaces, peaks)


def solution(mesh):
    in_specs = (
        P(("groups", "sect"), "tile", "half", None, None),
        P(None, ("groups", "sect"), "tile", "half"),
        P(None, ("groups", "sect"), "tile", "half"),
    )
    out_specs = (
        P(("groups", "sect"), "tile", "half", None, None),
        P(("groups", "sect"), "tile", "half"),
    )
    return jax.shard_map(body, mesh=mesh, in_specs=in_specs, out_specs=out_specs, check_vma=False)
```

```python
import functools

import jax
import jax.numpy as jnp
import numpy as np
from jax import lax
from jax.experimental import pallas as pl
from jax.experimental.pallas import tpu as pltpu
from jax.sharding import PartitionSpec as P

FLOOR = 0.05
STEPS = 32767.0
SMALLEST = 1.2e-34
MESH = pl.DeviceIdType.MESH


def real_tables(length):
    half = length // 2
    spots = np.arange(length)
    waves = np.arange(half)
    angles = (spots[:, None] * waves[None, :] % length) * (2.0 * np.pi / length)
    sines = np.sin(angles)
    sines[:, 0] = np.cos(np.pi * spots)
    table = np.concatenate([np.cos(angles), sines], axis=1).astype(np.float32)
    upper = table.astype(jnp.bfloat16)
    lower = (table - upper.astype(np.float32)).astype(jnp.bfloat16)
    column = np.stack([upper, lower])
    row = np.stack([upper.T, lower.T])
    return jnp.asarray(column), jnp.asarray(row)


def halves_of(value):
    upper = value.astype(jnp.bfloat16)
    return upper, (value - upper.astype(jnp.float32)).astype(jnp.bfloat16)


def dot(left, right):
    return jnp.dot(left, right, preferred_element_type=jnp.float32)


def left_product(table_ref, value):
    upper, lower = halves_of(value)
    return dot(table_ref[0], upper) + dot(table_ref[0], lower) + dot(table_ref[1], upper)


def right_product(value, table_ref):
    upper, lower = halves_of(value)
    return dot(upper, table_ref[0]) + dot(lower, table_ref[0]) + dot(upper, table_ref[1])


def packed_spectrum(picture, column_ref, row_ref):
    across = dot(picture, column_ref[0]) + dot(picture, column_ref[1])
    return left_product(row_ref, across)


def unpacked(packed, on_row, on_column):
    half = packed.shape[0] // 2
    cc, cs = packed[:half, :half], packed[:half, half:]
    sc, ss = packed[half:, :half], packed[half:, half:]
    edge = on_row | on_column
    plus_re = jnp.where(edge, cc, cc - ss)
    plus_im = jnp.where(on_row, cs, jnp.where(on_column, sc, sc + cs))
    minus_re = jnp.where(on_row, sc, jnp.where(on_column, cs, cc + ss))
    minus_im = jnp.where(edge, ss, cs - sc)
    return (plus_re, plus_im, minus_re, minus_im)


def phases(first_re, first_im, second_re, second_im, floor):
    cross_re = first_re * second_re + first_im * second_im
    cross_im = first_re * second_im - first_im * second_re
    power = cross_re * cross_re + cross_im * cross_im
    factor = jnp.minimum(lax.rsqrt(power), 1.0 / floor)
    return (cross_re * factor, cross_im * factor)


def correlate(first, second, column_ref, row_ref):
    length = first.shape[-1]
    half = length // 2
    floor = FLOOR * length * length
    first_packed = packed_spectrum(first, column_ref, row_ref)
    second_packed = packed_spectrum(second, column_ref, row_ref)
    rows = lax.broadcasted_iota(jnp.int32, (half, half), 0)
    columns = lax.broadcasted_iota(jnp.int32, (half, half), 1)
    on_row, on_column = rows == 0, columns == 0
    corner = on_row & on_column
    one = unpacked(first_packed, on_row, on_column)
    two = unpacked(second_packed, on_row, on_column)
    plus_re, plus_im = phases(one[0], one[1], two[0], two[1], floor)
    minus_re, minus_im = phases(one[2], one[3], two[2], two[3], floor)
    cc = jnp.where(on_row | on_column, plus_re, plus_re + minus_re)
    ss = jnp.where(on_row | on_column, -minus_im, minus_re - plus_re)
    sc = jnp.where(on_row, minus_re, jnp.where(on_column, -plus_im, minus_im - plus_im))
    cs = jnp.where(on_row, -plus_im, jnp.where(on_column, minus_re, -plus_im - minus_im))

    def at_corner(value, top, left):
        product = (
            first_packed[top : top + half, left : left + half]
            * second_packed[top : top + half, left : left + half]
        )
        real = product / jnp.maximum(jnp.abs(product), floor)
        return jnp.where(corner, 0.5 * real, value)

    packed = jnp.concatenate(
        [
            jnp.concatenate([at_corner(cc, 0, 0), at_corner(cs, 0, half)], axis=1),
            jnp.concatenate([at_corner(sc, half, 0), at_corner(ss, half, half)], axis=1),
        ],
        axis=0,
    )
    scale = 2.0 / length
    return left_product(column_ref, right_product(packed * scale, row_ref))


def slot_of(plan_ref, target, position):
    def look(slot, carried):
        seen, chosen, used = carried
        hit = (plan_ref[0, 0, 0, slot] == target).astype(jnp.int32)
        match = hit * (seen == position).astype(jnp.int32)
        return (seen + hit, chosen + match * slot, used + match)

    zero = jnp.int32(0)
    slots = plan_ref.shape[-1]
    _, chosen, used = lax.fori_loop(0, slots, look, (zero, zero, zero), unroll=True)
    return chosen, used


def stitch_kernel(
    sizes,
    lists_ref,
    plan_ref,
    patches_ref,
    column_ref,
    row_ref,
    surface_ref,
    peak_ref,
    own_ref,
    above_lists_ref,
    above_plan_ref,
    before_lists_ref,
    before_plan_ref,
    to_above_ref,
    to_before_ref,
    below_ref,
    next_ref,
    sent_ref,
    sent_note_ref,
    got_ref,
    got_note_ref,
    load_sem,
    list_send,
    list_recv,
    fetch_send,
    fetch_recv,
    code_send,
    code_recv,
    note_send,
    note_recv,
):
    tiles, sections, per_peer, works = sizes
    tile, sect = lax.axis_index("tile"), lax.axis_index("sect")
    lanes = tiles * per_peer

    load = pltpu.make_async_copy(patches_ref.at[0, 0], own_ref, load_sem)
    load.start()
    barrier = pltpu.get_barrier_semaphore()
    for shift in range(1, tiles):
        pl.semaphore_signal(
            barrier, inc=1, device_id={"tile": lax.rem(tile + shift, tiles)}, device_id_type=MESH
        )

    @pl.when(sect > 0)
    def _():
        pl.semaphore_signal(barrier, inc=1, device_id={"sect": sect - 1}, device_id_type=MESH)

    @pl.when(sect < sections - 1)
    def _():
        pl.semaphore_signal(barrier, inc=1, device_id={"sect": sect + 1}, device_id_type=MESH)

    neighbours = lax.min(sect, 1) + lax.min(sections - 1 - sect, 1)
    pl.semaphore_wait(barrier, tiles - 1 + neighbours)

    def list_copies(axis, place, refs, first_sem):
        return [
            pltpu.make_async_remote_copy(
                src_ref=source,
                dst_ref=target,
                send_sem=list_send.at[first_sem + index],
                recv_sem=list_recv.at[first_sem + index],
                device_id={axis: place},
                device_id_type=MESH,
            )
            for index, (source, target) in enumerate(zip((lists_ref, plan_ref), refs))
        ]

    to_below = list_copies(
        "tile", lax.min(tile + 1, tiles - 1), (above_lists_ref, above_plan_ref), 0
    )
    to_next = list_copies(
        "sect", lax.min(sect + 1, sections - 1), (before_lists_ref, before_plan_ref), 2
    )

    @pl.when(tile < tiles - 1)
    def _():
        for copy in to_below:
            copy.start()

    @pl.when(sect < sections - 1)
    def _():
        for copy in to_next:
            copy.start()

    surface_ref[...] = jnp.zeros_like(surface_ref)
    peak_ref[...] = jnp.zeros_like(peak_ref)
    load.wait()

    def target_of(owner_tile, lane):
        block = lane // per_peer
        passed = lax.max(lax.min(block - owner_tile + 1, 1), 0)
        return block + passed - (tiles - owner_tile) * (block // (tiles - 1))

    def to_above(lane):
        return pltpu.make_async_remote_copy(
            src_ref=to_above_ref.at[lane],
            dst_ref=below_ref.at[lane],
            send_sem=fetch_send.at[0, lane],
            recv_sem=fetch_recv.at[0, lane],
            device_id={"tile": lax.max(tile - 1, 0)},
            device_id_type=MESH,
        )

    def to_before(lane):
        return pltpu.make_async_remote_copy(
            src_ref=to_before_ref.at[lane],
            dst_ref=next_ref.at[lane],
            send_sem=fetch_send.at[1, lane],
            recv_sem=fetch_recv.at[1, lane],
            device_id={"sect": lax.max(sect - 1, 0)},
            device_id_type=MESH,
        )

    @pl.when(tile > 0)
    def _():
        for copy in to_below:
            copy.wait_recv()

        def stage(lane, carried):
            slot, _ = slot_of(
                above_plan_ref, target_of(tile - 1, lane), lax.rem(lane, per_peer)
            )
            to_above_ref[lane] = own_ref[above_lists_ref[2, 0, 0, slot]]
            return carried

        lax.fori_loop(0, lanes, stage, 0)

        def send(lane, carried):
            to_above(lane).start()
            return carried

        lax.fori_loop(0, lanes, send, 0)

    @pl.when(sect > 0)
    def _():
        for copy in to_next:
            copy.wait_recv()

        def stage(lane, carried):
            slot, _ = slot_of(before_plan_ref, target_of(tile, lane), lax.rem(lane, per_peer))
            to_before_ref[lane] = own_ref[before_lists_ref[2, 0, 0, slot]]
            return carried

        lax.fori_loop(0, lanes, stage, 0)

        def send(lane, carried):
            to_before(lane).start()
            return carried

        lax.fori_loop(0, lanes, send, 0)

    def copies(lane, target, place):
        code = pltpu.make_async_remote_copy(
            src_ref=sent_ref.at[lane],
            dst_ref=got_ref.at[place],
            send_sem=code_send.at[lane],
            recv_sem=code_recv.at[place],
            device_id={"tile": target},
            device_id_type=MESH,
        )
        note = pltpu.make_async_remote_copy(
            src_ref=sent_note_ref.at[lane],
            dst_ref=got_note_ref.at[place],
            send_sem=note_send.at[lane],
            recv_sem=note_recv.at[place],
            device_id={"tile": target},
            device_id_type=MESH,
        )
        return code, note

    slot_ids = lax.broadcasted_iota(jnp.int32, peak_ref.shape, 2)

    def settle(code, note):
        found = code.astype(jnp.int32).astype(jnp.float32) * note[0:1]
        place = note[1:2]
        for work in range(works):
            surface_ref[0, 0, work] = jnp.where(
                place == float(work), found, surface_ref[0, 0, work]
            )

    def correlate_lane(lane, carried):
        target = target_of(tile, lane)
        slot, used = slot_of(plan_ref, target, lax.rem(lane, per_peer))
        kind = lists_ref[0, 0, 0, slot]
        first = own_ref[lists_ref[1, 0, 0, slot]]

        @pl.when(tile < tiles - 1)
        def _():
            to_above(lane).wait_recv()

        @pl.when(sect < sections - 1)
        def _():
            to_before(lane).wait_recv()

        second = jnp.where(kind == 0, below_ref[lane], next_ref[lane])
        surface = correlate(first, second, column_ref, row_ref)
        peak = jnp.max(surface)
        peak_ref[...] = jnp.where(
            (slot_ids == slot) & (used > 0), jnp.full(peak_ref.shape, peak), peak_ref[...]
        )
        place = jnp.where(used > 0, plan_ref[1, 0, 0, slot], -1).astype(jnp.float32)
        tallest = jnp.max(jnp.abs(surface), axis=0, keepdims=True)
        tallest = jnp.maximum(tallest, SMALLEST)
        code = jnp.round(surface * (STEPS / tallest)).astype(jnp.int32).astype(jnp.int16)
        sent_ref[lane] = code
        note_row = lax.broadcasted_iota(jnp.int32, sent_note_ref.shape[1:], 0)
        sent_note_ref[lane] = jnp.where(note_row == 0, tallest * (1.0 / STEPS), place)

        @pl.when(lane < lanes - per_peer)
        def _():
            code_copy, note_copy = copies(
                lane, target, tile * per_peer + lax.rem(lane, per_peer)
            )
            note_copy.start()
            code_copy.start()

        return carried

    lax.fori_loop(0, lanes, correlate_lane, 0)

    def settle_own(lane, carried):
        settle(sent_ref[lane], sent_note_ref[lane])
        return carried

    lax.fori_loop(lanes - per_peer, lanes, settle_own, 0)

    def settle_lane(lane, carried):
        source = target_of(tile, lane)
        place = source * per_peer + lax.rem(lane, per_peer)
        code_copy, note_copy = copies(lane, source, place)
        note_copy.wait()
        code_copy.wait()
        settle(got_ref[place], got_note_ref[place])
        return carried

    lax.fori_loop(0, lanes - per_peer, settle_lane, 0)

    def patches_left(lane, carried):
        @pl.when(tile > 0)
        def _():
            to_above(lane).wait_send()

        @pl.when(sect > 0)
        def _():
            to_before(lane).wait_send()

        return carried

    lax.fori_loop(0, lanes, patches_left, 0)

    @pl.when(tile < tiles - 1)
    def _():
        for copy in to_below:
            copy.wait_send()

    @pl.when(sect < sections - 1)
    def _():
        for copy in to_next:
            copy.wait_send()


def body(patches, pair_lists, move_plan):
    length = patches.shape[-1]
    slots = pair_lists.shape[-1]
    works = slots // 2
    tiles, sections = lax.axis_size("tile"), lax.axis_size("sect")
    per_peer = (slots + tiles - 1) // tiles
    lanes = tiles * per_peer
    column, row = real_tables(length)
    vmem = pl.BlockSpec(memory_space=pltpu.VMEM)
    smem = pl.BlockSpec(memory_space=pltpu.SMEM)
    surfaces, peaks = pl.pallas_call(
        functools.partial(stitch_kernel, (tiles, sections, per_peer, works)),
        in_specs=[smem, smem, pl.BlockSpec(memory_space=pl.ANY), vmem, vmem],
        out_specs=[vmem, vmem],
        out_shape=[
            jax.ShapeDtypeStruct((1, 1, works, length, length), jnp.float32),
            jax.ShapeDtypeStruct((1, 1, slots), jnp.float32),
        ],
        scratch_shapes=[
            pltpu.VMEM(patches.shape[2:], jnp.bfloat16),
            pltpu.SMEM(pair_lists.shape, jnp.int32),
            pltpu.SMEM(move_plan.shape, jnp.int32),
            pltpu.SMEM(pair_lists.shape, jnp.int32),
            pltpu.SMEM(move_plan.shape, jnp.int32),
            pltpu.VMEM((lanes, length, length), jnp.bfloat16),
            pltpu.VMEM((lanes, length, length), jnp.bfloat16),
            pltpu.VMEM((lanes, length, length), jnp.bfloat16),
            pltpu.VMEM((lanes, length, length), jnp.bfloat16),
            pltpu.VMEM((lanes, length, length), jnp.int16),
            pltpu.VMEM((lanes, 2, length), jnp.float32),
            pltpu.VMEM((lanes, length, length), jnp.int16),
            pltpu.VMEM((lanes, 2, length), jnp.float32),
            pltpu.SemaphoreType.DMA(()),
            pltpu.SemaphoreType.DMA((4,)),
            pltpu.SemaphoreType.DMA((4,)),
            pltpu.SemaphoreType.DMA((2, lanes)),
            pltpu.SemaphoreType.DMA((2, lanes)),
            pltpu.SemaphoreType.DMA((lanes,)),
            pltpu.SemaphoreType.DMA((lanes,)),
            pltpu.SemaphoreType.DMA((lanes,)),
            pltpu.SemaphoreType.DMA((lanes,)),
        ],
        compiler_params=pltpu.CompilerParams(collective_id=0, has_side_effects=True),
    )(pair_lists, move_plan, patches, column, row)
    return (surfaces, peaks)


def solution(mesh):
    in_specs = (
        P(("groups", "sect"), "tile", "half", None, None),
        P(None, ("groups", "sect"), "tile", "half"),
        P(None, ("groups", "sect"), "tile", "half"),
    )
    out_specs = (
        P(("groups", "sect"), "tile", "half", None, None),
        P(("groups", "sect"), "tile", "half"),
    )
    return jax.shard_map(body, mesh=mesh, in_specs=in_specs, out_specs=out_specs, check_vma=False)
```
